32 devices in a mesh: row: 4 (over x, core), col: 8 (over z, y).
Axes of the slice: x: 2, y: 2, z: 4, core: 2. Of those that a mesh axis runs over, the one named last changes fastest.
Arguments:
- blocks: float32 [256, 8, 128, 128], P(('row', 'col')), may hold values from -2 to 2
- prolong: float32 [256, 128, 128], P(('row', 'col')), may hold values from -0.5 to 0.5
- counts: int32 [256], P(('row', 'col')), may hold values from 1 to 8
- columns: int32 [256, 8], P(('row', 'col')), may hold values from 0 to 63, as said below
- aggregates: int32 [256], P(('row', 'col')), may hold values from 0 to 1
Outputs:
- coarse_operator: float32 [64, 16, 128, 128], P(('row', 'col'))
The draws below stay inside these ranges and needn't reach their ends.
Inputs may be any that keep to these rules, and one draw needn't show every extreme that they name: Over all slots of the 8 rows of one device, the columns that fall among the rows of any one device of the slab (columns // 8 equal) take at most 2 distinct values; every device reaches 2 for some such device.
All inputs are finite; a program needn't handle non-finite values.
Results may differ from the reference program's by a relative error of at most 0.0003.
Values sent between devices are 32-bit elements; how exact they have to be, the bound alone decides.
A program may use at most 64 MiB of HBM per device.

```python
import jax
import jax.numpy as jnp
from jax import lax

TB = 128
K = 8
BR = 8
AGD = 2
CAP = 2
NB = 256
N_COL = 8


def draw_columns(key, part):
    key_owner = jax.random.fold_in(key, 11)
    key_base = jax.random.fold_in(key, 12)
    key_offset = jax.random.fold_in(key, 13)
    owner = jax.random.randint(key_owner, (NB, K), 0, N_COL, dtype=jnp.int32)
    offset = jax.random.randint(key_offset, (NB, K), 0, CAP, dtype=jnp.int32)
    base = jax.random.randint(key_base, (NB // BR, N_COL), 0, BR, dtype=jnp.int32)
    base_rows = jnp.repeat(base, BR, axis=0)
    first_row = jnp.arange(NB, dtype=jnp.int32) % BR == 0
    first_slots = jnp.arange(K, dtype=jnp.int32) < CAP
    forced = first_row[:, None] & first_slots[None, :]
    owner = jnp.where(forced, owner[:, :1], owner)
    offset = jnp.where(forced, jnp.arange(K, dtype=jnp.int32)[None, :], offset)
    chosen = jnp.take_along_axis(base_rows, owner, axis=1)
    local = (chosen + offset) % BR
    return (owner * BR + local).astype(jnp.int32)


def place_ends(entries, stream_key, smallest, largest):
    longest = entries.shape.index(max(entries.shape))
    spots = []
    for shift in (0, 1):
        where = [jax.random.randint(jax.random.fold_in(stream_key, axis), (), 0, length) for axis, length in enumerate(entries.shape)]
        where[longest] = (where[longest] + shift) % entries.shape[longest]
        spots.append(tuple(where))
    return entries.at[spots[0]].set(smallest).at[spots[1]].set(largest)


def block_scale(key, dims, shards, low, top_value):
    level, own = 1.0, jax.random.fold_in(key, 6)
    for axis_at, blocks in shards:
        steps = jnp.exp(jax.random.uniform(jax.random.fold_in(own, axis_at), (blocks,), jnp.float32, low / len(shards), top_value / len(shards)))
        level = level * jnp.repeat(steps, dims[axis_at] // blocks).reshape([-1 if axis == axis_at else 1 for axis in range(len(dims))])
    return level


def bell_draw(rng, extent, width, most, pieces=(), kind=jnp.bfloat16):
    drawn = jax.random.normal(rng, extent, jnp.float32) * width
    if len(pieces) > 0:
        drawn = block_scale(rng, extent, pieces, -0.22, 0.18) * drawn
    return jnp.clip(drawn, min=-most, max=most).astype(kind)


def setup_inputs(seed: int = 0) -> dict:
    arg_keys = jax.random.split(jax.random.key(seed), 6)
    blocks = bell_draw(arg_keys[0], (NB, K, TB, TB), 0.25, 2.0, ((0, 32),), jnp.float32)
    prolong = bell_draw(arg_keys[1], (NB, TB, TB), TB ** -0.5, 0.5, ((0, 32),), jnp.float32)
    counts = place_ends(jax.random.randint(arg_keys[2], (NB,), 1, K + 1), jax.random.fold_in(arg_keys[2], 1), 1, K).astype(jnp.int32)
    columns = draw_columns(jax.random.fold_in(arg_keys[5], 71), 0)
    aggregates = place_ends(jax.random.randint(arg_keys[4], (NB,), 0, AGD), jax.random.fold_in(arg_keys[4], 1), 0, AGD - 1).astype(jnp.int32)
    return {"blocks": blocks, "prolong": prolong, "counts": counts, "columns": columns, "aggregates": aggregates}


def reference(blocks, prolong, counts, columns, aggregates):
    fine = BR * N_COL
    wide = AGD * N_COL
    slots = blocks.shape[1]
    tile = blocks.shape[-1]
    groups = blocks.shape[0] // BR
    high = lax.Precision.HIGHEST

    def one_group(group):
        start = (group * BR).astype(jnp.int32)
        tiles = lax.dynamic_slice_in_dim(blocks, start, BR, 0)
        own = lax.dynamic_slice_in_dim(prolong, start, BR, 0)
        live_count = lax.dynamic_slice_in_dim(counts, start, BR, 0)
        cols = lax.dynamic_slice_in_dim(columns, start, BR, 0)
        own_agg = lax.dynamic_slice_in_dim(aggregates, start, BR, 0)
        base = ((group // N_COL) * fine).astype(jnp.int32)
        joined = (base + cols).astype(jnp.int32)
        picked = jnp.take(prolong, joined, axis=0)
        col_agg = jnp.take(aggregates, joined, axis=0)
        coarse_col = (cols // BR) * AGD + col_agg
        inner = jnp.einsum('bkxy,bkyz->bkxz', tiles, picked, precision=high)
        terms = jnp.einsum('bxw,bkxz->bkwz', own, inner, precision=high)
        live = (jnp.arange(slots, dtype=jnp.int32)[None, :] < live_count[:, None]).astype(blocks.dtype)
        col_hot = (coarse_col[:, :, None] == jnp.arange(wide, dtype=jnp.int32)[None, None, :]).astype(blocks.dtype) * live[:, :, None]
        row_hot = (own_agg[:, None] == jnp.arange(AGD, dtype=jnp.int32)[None, :]).astype(blocks.dtype)
        weights = (row_hot[:, None, :, None] * col_hot[:, :, None, :]).reshape(BR * slots, AGD * wide)
        flat_terms = terms.reshape(BR * slots, tile * tile)
        summed = jnp.dot(weights.T, flat_terms, precision=high)
        return summed.reshape(AGD, wide, tile, tile)

    galerkin = lax.map(one_group, jnp.arange(groups, dtype=jnp.int32))
    galerkin = galerkin.reshape(groups * AGD, wide, tile, tile)
    sums = jnp.sum(jnp.abs(galerkin), axis=(1, 3))
    bound = jnp.max(sums)
    return galerkin / (bound + 1e-6)
```

```python
import functools

import jax
import jax.numpy as jnp
from jax import lax
from jax.experimental import pallas as pl
from jax.experimental.pallas import tpu as pltpu
from jax.sharding import PartitionSpec as P

AGD = 2
CAP = 2
F32 = jnp.float32
BF16 = jnp.bfloat16
I32 = jnp.int32


def halves(x):
    high = x.astype(BF16)
    return high, (x - high.astype(F32)).astype(BF16)


def dot(a, b):
    return jnp.dot(a, b, preferred_element_type=F32)


def kernel(
    n, m, blocks_ref, prolong_ref, cols_v, agg_v, cols_s, agg_s, counts_s,
    out_ref, bound_ref,
    blocks, prolong, partial, table, sent, got, cols_all, agg_all, rowsum, peak, peaks_col,
    peak2, peaks_row, table_s,
    block_sem, prolong_sem, table_sem, cols_send, cols_recv, agg_send, agg_recv,
    tile_send, tile_recv, pc_send, pc_recv, pr_send, pr_recv,
):
    rows, slots = cols_v.shape
    tile = prolong.shape[-1]
    none = rows * slots
    me = lax.axis_index("col")
    my_row = lax.axis_index("row")

    load_prolong = pltpu.make_async_copy(prolong_ref, prolong, prolong_sem)
    load_prolong.start()

    def load_block(i):
        return pltpu.make_async_copy(blocks_ref.at[i], blocks.at[i], block_sem.at[i])

    @pl.loop(0, rows)
    def _(i):
        load_block(i).start()

    def across(off):
        return lax.rem(me + off, n)

    def below(off):
        return lax.rem(my_row + off, m)

    barrier = pltpu.get_barrier_semaphore()

    @pl.loop(1, n)
    def _(off):
        pl.semaphore_signal(barrier, inc=1, device_id={"col": across(off)})

    @pl.loop(1, m)
    def _(off):
        pl.semaphore_signal(barrier, inc=1, device_id={"row": below(off)})

    pl.semaphore_wait(barrier, n + m - 2)

    def far_first(t):
        return n // 2 + (lax.rem(t, 2) * 2 - 1) * (t // 2)

    def send_cols(to, slot):
        return pltpu.make_async_remote_copy(
            cols_v, cols_all.at[slot], cols_send.at[to], cols_recv.at[slot], device_id={"col": to}
        )

    def send_agg(to, slot):
        return pltpu.make_async_remote_copy(
            agg_v, agg_all.at[slot], agg_send.at[to], agg_recv.at[slot], device_id={"col": to}
        )

    @pl.loop(1, n)
    def _(t):
        to = across(far_first(t))
        send_cols(to, me).start()
        send_agg(to, me).start()

    sub = lax.broadcasted_iota(I32, (8, 128), 0)
    lane = lax.broadcasted_iota(I32, (8, 128), 1)
    keys = jnp.full((8, 128), -1, I32)
    for i in range(rows):
        for k in range(slots):
            here = (sub == i) & (lane == k)
            keys = jnp.where(here, cols_s[i, k] * AGD + agg_s[i], keys)
    order = sub * slots + lane

    def scan_keys(i, carry):
        prev, low, high = carry
        for k in range(slots):
            col = cols_s[i, k]
            s = i * slots + k
            owner, within = col // rows, lax.rem(col, rows)
            key = jnp.where(k < counts_s[i], col * AGD + agg_s[i], -2)
            prev = jnp.where((keys == key) & (order > s), s, prev)
            low = jnp.where(lane == owner, jnp.minimum(low, within), low)
            high = jnp.where(lane == owner, jnp.maximum(high, within), high)
        return prev, low, high

    prev, low, high = lax.fori_loop(
        0, rows, scan_keys,
        (jnp.full((8, 128), none, I32), jnp.full((8, 128), rows - 1, I32), jnp.zeros((8, 128), I32)),
    )
    wanted = jnp.where(lax.rem(sub, 2) == 0, low, jnp.where(high > low, high, -1))

    def scan_last(i, last):
        for k in range(slots):
            col = cols_s[i, k]
            owner, within = col // rows, lax.rem(col, rows)
            row = jnp.where(k < counts_s[i], agg_s[i], -1)
            hit = (lane == owner) & (sub // 2 == row) & (wanted == within)
            last = jnp.where(hit, i * slots + k, last)
        return last

    last = lax.fori_loop(0, rows, scan_last, jnp.full((8, 128), none, I32))
    table[0:8, :] = prev
    table[8:16, :] = last
    table[16:24, :] = jnp.where(sub == 0, low, high)
    to_scalars = pltpu.make_async_copy(table, table_s, table_sem)
    to_scalars.start()
    partial[none] = jnp.zeros((tile, tile), F32)
    agg_all[me] = agg_v[...]
    to_scalars.wait()

    load_prolong.wait()
    got[me, 0] = prolong[table_s[16, me]]
    got[me, 1] = prolong[table_s[17, me]]

    def send_tiles(to, slot):
        return pltpu.make_async_remote_copy(
            sent.at[to], got.at[slot], tile_send.at[to], tile_recv.at[slot], device_id={"col": to}
        )

    def reply(t, _):
        to = across(far_first(t))
        send_cols(to, to).wait_recv()
        asked = cols_all[to]
        mine = asked // rows == me
        within = lax.rem(asked, rows)
        sent[to, 0] = prolong[jnp.min(jnp.where(mine, within, rows - 1))]
        sent[to, 1] = prolong[jnp.max(jnp.where(mine, within, 0))]
        send_tiles(to, me).start()
        return 0

    lax.fori_loop(1, n, reply, 0)

    def first_product(i, _):
        load_block(i).wait()
        ph, pw = halves(prolong[i].T)
        lhs = jnp.concatenate([ph, pw, ph], axis=1)
        for k in range(0, slots, 2):
            ah, aw = halves(blocks[i, k])
            bh, bw = halves(blocks[i, k + 1])
            highs = jnp.concatenate([ah, bh], axis=1)
            rhs = jnp.concatenate([highs, highs, jnp.concatenate([aw, bw], axis=1)], axis=0)
            both = dot(lhs, rhs)
            s = i * slots + k
            partial[s] = both[:, :tile] + partial[table_s[i, k]]
            partial[s + 1] = both[:, tile:] + partial[table_s[i, k + 1]]
        return 0

    lax.fori_loop(0, rows, first_product, 0)

    rowsum[...] = jnp.zeros_like(rowsum)
    spot = lax.broadcasted_iota(I32, agg_v.shape, 1)

    def second_product(owner):
        lhs = jnp.concatenate(
            [
                jnp.concatenate([partial[table_s[8 + c * CAP + r, owner]] for r in range(CAP)], axis=1)
                for c in range(AGD)
            ],
            axis=0,
        )
        ids = agg_all[owner]
        right = []
        for r in range(CAP):
            one = jnp.max(jnp.where(spot == table_s[16 + r, owner], ids, 0)).astype(F32)
            p = got[owner, r]
            right.append(jnp.concatenate([p * (1.0 - one), p * one], axis=1))
        rhs = jnp.concatenate(right, axis=0)
        lh, lw = halves(lhs)
        rh, rw = halves(rhs)
        prod = dot(lh, rh) + dot(lh, rw) + dot(lw, rh)
        size = jnp.abs(prod)
        rowsum[...] += size[:, :tile] + size[:, tile:]
        for c in range(AGD):
            for a in range(AGD):
                out_ref[c, owner * AGD + a] = prod[
                    c * tile : (c + 1) * tile, a * tile : (a + 1) * tile
                ]

    second_product(me)

    def collect(t, _):
        owner = lax.rem(me - far_first(t) + n, n)
        send_agg(owner, owner).wait_recv()
        send_tiles(owner, owner).wait_recv()
        second_product(owner)
        return 0

    lax.fori_loop(1, n, collect, 0)

    most = jnp.max(jnp.sum(rowsum[...], axis=1, keepdims=True), axis=0, keepdims=True)
    peak[...] = jnp.broadcast_to(most, peak.shape)
    peaks_col[me] = jnp.broadcast_to(most, peak.shape)

    def send_peak(to, slot):
        return pltpu.make_async_remote_copy(
            peak, peaks_col.at[slot], pc_send.at[to], pc_recv.at[slot], device_id={"col": to}
        )

    def send_peak2(to, slot):
        return pltpu.make_async_remote_copy(
            peak2, peaks_row.at[slot], pr_send.at[to], pr_recv.at[slot], device_id={"row": to}
        )

    @pl.loop(1, n)
    def _(t):
        send_peak(across(far_first(t)), me).start()

    @pl.loop(1, n)
    def _(off):
        to = across(off)
        send_cols(to, me).wait_send()
        send_agg(to, me).wait_send()
        send_tiles(to, me).wait_send()

    @pl.loop(1, n)
    def _(off):
        send_peak(across(off), across(off)).wait_recv()

    over = jnp.max(peaks_col[...], axis=0)
    peak2[...] = over
    peaks_row[my_row] = over

    @pl.loop(1, m)
    def _(off):
        send_peak2(below(off), my_row).start()

    @pl.loop(1, m)
    def _(off):
        send_peak2(below(off), below(off)).wait_recv()

    bound_ref[...] = jnp.max(peaks_row[...], axis=0)

    @pl.loop(1, n)
    def _(off):
        send_peak(across(off), me).wait_send()

    @pl.loop(1, m)
    def _(off):
        send_peak2(below(off), my_row).wait_send()


def per_device(blocks, prolong, counts, columns, aggregates):
    rows, slots, tile, _ = blocks.shape
    n, m = lax.axis_size("col"), lax.axis_size("row")
    agg_row = aggregates.reshape(1, rows)
    dma = pltpu.SemaphoreType.DMA
    vmem = pl.BlockSpec(memory_space=pltpu.VMEM)
    smem = pl.BlockSpec(memory_space=pltpu.SMEM)
    anywhere = pl.BlockSpec(memory_space=pl.ANY)
    galerkin, bound = pl.pallas_call(
        functools.partial(kernel, n, m),
        name="galerkin",
        out_shape=(
            jax.ShapeDtypeStruct((AGD, AGD * n, tile, tile), F32),
            jax.ShapeDtypeStruct((8, 128), F32),
        ),
        in_specs=[anywhere, anywhere, vmem, vmem, smem, smem, smem],
        out_specs=(vmem, vmem),
        scratch_shapes=[
            pltpu.VMEM((rows, slots, tile, tile), F32),
            pltpu.VMEM((rows, tile, tile), F32),
            pltpu.VMEM((rows * slots + 1, tile, tile), F32),
            pltpu.VMEM((24, 128), I32),
            pltpu.VMEM((n, CAP, tile, tile), F32),
            pltpu.VMEM((n, CAP, tile, tile), F32),
            pltpu.VMEM((n, rows, slots), I32),
            pltpu.VMEM((n, 1, rows), I32),
            pltpu.VMEM((AGD * tile, tile), F32),
            pltpu.VMEM((8, 128), F32),
            pltpu.VMEM((n, 8, 128), F32),
            pltpu.VMEM((8, 128), F32),
            pltpu.VMEM((m, 8, 128), F32),
            pltpu.SMEM((24, 128), I32),
            dma((rows,)),
            dma,
            dma,
        ]
        + [dma((n,)) for _ in range(8)]
        + [dma((m,)) for _ in range(2)],
        compiler_params=pltpu.CompilerParams(
            collective_id=0, has_side_effects=True, vmem_limit_bytes=48 * 1024 * 1024
        ),
    )(blocks, prolong, columns, agg_row, columns, aggregates, counts)
    return galerkin / (bound[0, 0] + 1e-06)


def solution(mesh):
    placed = (
        P(("row", "col"), None, None, None),
        P(("row", "col"), None, None),
        P(("row", "col")),
        P(("row", "col"), None),
        P(("row", "col")),
    )
    return jax.shard_map(
        per_device,
        mesh=mesh,
        in_specs=placed,
        out_specs=P(("row", "col"), None, None, None),
        check_vma=False,
    )
```

```python
import functools

import jax
import jax.numpy as jnp
from jax import lax
from jax.experimental import pallas as pl
from jax.experimental.pallas import tpu as pltpu
from jax.sharding import PartitionSpec as P

AGD = 2
CAP = 2
F32 = jnp.float32
BF16 = jnp.bfloat16
I32 = jnp.int32


def halves(x):
    high = x.astype(BF16)
    return high, (x - high.astype(F32)).astype(BF16)


def dot(a, b):
    return jnp.dot(a, b, preferred_element_type=F32)


def kernel(
    n, m, blocks_ref, prolong_ref, cols_ref, agg_ref, counts_ref,
    out_ref, bound_ref,
    cols_v, agg_v, cols_s, agg_s, counts_s, small_sem,
    blocks, prolong, partial, table, sent, got, cols_all, agg_all, rowsum, peak, peaks_col,
    peak2, peaks_row, table_s,
    block_sem, prolong_sem, table_sem, cols_send, cols_recv, agg_send, agg_recv,
    tile_send, tile_recv, pc_send, pc_recv, pr_send, pr_recv,
):
    rows, slots = cols_v.shape
    tile = prolong.shape[-1]
    none = rows * slots
    me = lax.axis_index("col")
    my_row = lax.axis_index("row")

    load_prolong = pltpu.make_async_copy(prolong_ref, prolong, prolong_sem)
    small = [
        pltpu.make_async_copy(src, dst, small_sem.at[at])
        for at, (src, dst) in enumerate(
            (
                (cols_ref, cols_v),
                (agg_ref, agg_v),
                (cols_ref, cols_s),
                (agg_ref, agg_s),
                (counts_ref, counts_s),
            )
        )
    ]
    for copy in small:
        copy.start()
    load_prolong.start()

    def load_block(i):
        return pltpu.make_async_copy(blocks_ref.at[i], blocks.at[i], block_sem.at[i])

    @pl.loop(0, rows)
    def _(i):
        load_block(i).start()

    def across(off):
        return lax.rem(me + off, n)

    def below(off):
        return lax.rem(my_row + off, m)

    barrier = pltpu.get_barrier_semaphore()

    @pl.loop(1, n)
    def _(off):
        pl.semaphore_signal(barrier, inc=1, device_id={"col": across(off)})

    @pl.loop(1, m)
    def _(off):
        pl.semaphore_signal(barrier, inc=1, device_id={"row": below(off)})

    for copy in small:
        copy.wait()
    pl.semaphore_wait(barrier, n + m - 2)

    def far_first(t):
        return n // 2 + (lax.rem(t, 2) * 2 - 1) * (t // 2)

    def send_cols(to, slot):
        return pltpu.make_async_remote_copy(
            cols_v, cols_all.at[slot], cols_send.at[to], cols_recv.at[slot], device_id={"col": to}
        )

    def send_agg(to, slot):
        return pltpu.make_async_remote_copy(
            agg_v, agg_all.at[slot], agg_send.at[to], agg_recv.at[slot], device_id={"col": to}
        )

    @pl.loop(1, n)
    def _(t):
        to = across(far_first(t))
        send_cols(to, me).start()
        send_agg(to, me).start()

    sub = lax.broadcasted_iota(I32, (8, 128), 0)
    lane = lax.broadcasted_iota(I32, (8, 128), 1)
    keys = jnp.full((8, 128), -1, I32)
    for i in range(rows):
        for k in range(slots):
            here = (sub == i) & (lane == k)
            keys = jnp.where(here, cols_s[i, k] * AGD + agg_s[0, i], keys)
    order = sub * slots + lane

    def scan_keys(i, carry):
        prev, low, high = carry
        for k in range(slots):
            col = cols_s[i, k]
            s = i * slots + k
            owner, within = col // rows, lax.rem(col, rows)
            key = jnp.where(k < counts_s[0, i], col * AGD + agg_s[0, i], -2)
            prev = jnp.where((keys == key) & (order > s), s, prev)
            low = jnp.where(lane == owner, jnp.minimum(low, within), low)
            high = jnp.where(lane == owner, jnp.maximum(high, within), high)
        return prev, low, high

    prev, low, high = lax.fori_loop(
        0, rows, scan_keys,
        (jnp.full((8, 128), none, I32), jnp.full((8, 128), rows - 1, I32), jnp.zeros((8, 128), I32)),
    )
    wanted = jnp.where(lax.rem(sub, 2) == 0, low, jnp.where(high > low, high, -1))

    def scan_last(i, last):
        for k in range(slots):
            col = cols_s[i, k]
            owner, within = col // rows, lax.rem(col, rows)
            row = jnp.where(k < counts_s[0, i], agg_s[0, i], -1)
            hit = (lane == owner) & (sub // 2 == row) & (wanted == within)
            last = jnp.where(hit, i * slots + k, last)
        return last

    last = lax.fori_loop(0, rows, scan_last, jnp.full((8, 128), none, I32))
    table[0:8, :] = prev
    table[8:16, :] = last
    table[16:24, :] = jnp.where(sub == 0, low, high)
    to_scalars = pltpu.make_async_copy(table, table_s, table_sem)
    to_scalars.start()
    partial[none] = jnp.zeros((tile, tile), F32)
    agg_all[me] = agg_v[...]
    to_scalars.wait()

    load_prolong.wait()
    got[me, 0] = prolong[table_s[16, me]]
    got[me, 1] = prolong[table_s[17, me]]

    def send_tiles(to, slot):
        return pltpu.make_async_remote_copy(
            sent.at[to], got.at[slot], tile_send.at[to], tile_recv.at[slot], device_id={"col": to}
        )

    def reply(t, _):
        to = across(far_first(t))
        send_cols(to, to).wait_recv()
        asked = cols_all[to]
        mine = asked // rows == me
        within = lax.rem(asked, rows)
        sent[to, 0] = prolong[jnp.min(jnp.where(mine, within, rows - 1))]
        sent[to, 1] = prolong[jnp.max(jnp.where(mine, within, 0))]
        send_tiles(to, me).start()
        return 0

    lax.fori_loop(1, n, reply, 0)

    def first_product(i, _):
        load_block(i).wait()
        ph, pw = halves(prolong[i].T)
        lhs = jnp.concatenate([ph, pw, ph], axis=1)
        for k in range(0, slots, 2):
            ah, aw = halves(blocks[i, k])
            bh, bw = halves(blocks[i, k + 1])
            highs = jnp.concatenate([ah, bh], axis=1)
            rhs = jnp.concatenate([highs, highs, jnp.concatenate([aw, bw], axis=1)], axis=0)
            both = dot(lhs, rhs)
            s = i * slots + k
            partial[s] = both[:, :tile] + partial[table_s[i, k]]
            partial[s + 1] = both[:, tile:] + partial[table_s[i, k + 1]]
        return 0

    lax.fori_loop(0, rows, first_product, 0)

    rowsum[...] = jnp.zeros_like(rowsum)
    spot = lax.broadcasted_iota(I32, agg_v.shape, 1)

    def second_product(owner):
        lhs = jnp.concatenate(
            [
                jnp.concatenate([partial[table_s[8 + c * CAP + r, owner]] for r in range(CAP)], axis=1)
                for c in range(AGD)
            ],
            axis=0,
        )
        ids = agg_all[owner]
        right = []
        for r in range(CAP):
            one = jnp.max(jnp.where(spot == table_s[16 + r, owner], ids, 0)).astype(F32)
            p = got[owner, r]
            right.append(jnp.concatenate([p * (1.0 - one), p * one], axis=1))
        rhs = jnp.concatenate(right, axis=0)
        lh, lw = halves(lhs)
        rh, rw = halves(rhs)
        prod = dot(lh, rh) + dot(lh, rw) + dot(lw, rh)
        size = jnp.abs(prod)
        rowsum[...] += size[:, :tile] + size[:, tile:]
        for c in range(AGD):
            for a in range(AGD):
                out_ref[c, owner * AGD + a] = prod[
                    c * tile : (c + 1) * tile, a * tile : (a + 1) * tile
                ]

    second_product(me)

    def collect(t, _):
        owner = lax.rem(me - far_first(t) + n, n)
        send_agg(owner, owner).wait_recv()
        send_tiles(owner, owner).wait_recv()
        second_product(owner)
        return 0

    lax.fori_loop(1, n, collect, 0)

    most = jnp.max(jnp.sum(rowsum[...], axis=1, keepdims=True), axis=0, keepdims=True)
    peak[...] = jnp.broadcast_to(most, peak.shape)
    peaks_col[me] = jnp.broadcast_to(most, peak.shape)

    def send_peak(to, slot):
        return pltpu.make_async_remote_copy(
            peak, peaks_col.at[slot], pc_send.at[to], pc_recv.at[slot], device_id={"col": to}
        )

    def send_peak2(to, slot):
        return pltpu.make_async_remote_copy(
            peak2, peaks_row.at[slot], pr_send.at[to], pr_recv.at[slot], device_id={"row": to}
        )

    @pl.loop(1, n)
    def _(t):
        send_peak(across(far_first(t)), me).start()

    @pl.loop(1, n)
    def _(off):
        to = across(off)
        send_cols(to, me).wait_send()
        send_agg(to, me).wait_send()
        send_tiles(to, me).wait_send()

    @pl.loop(1, n)
    def _(off):
        send_peak(across(off), across(off)).wait_recv()

    over = jnp.max(peaks_col[...], axis=0)
    peak2[...] = over
    peaks_row[my_row] = over

    @pl.loop(1, m)
    def _(off):
        send_peak2(below(off), my_row).start()

    @pl.loop(1, m)
    def _(off):
        send_peak2(below(off), below(off)).wait_recv()

    bound_ref[...] = jnp.broadcast_to(jnp.max(peaks_row[...], axis=0)[:1, :1], bound_ref.shape)

    @pl.loop(1, n)
    def _(off):
        send_peak(across(off), me).wait_send()

    @pl.loop(1, m)
    def _(off):
        send_peak2(below(off), my_row).wait_send()


def per_device(blocks, prolong, counts, columns, aggregates):
    rows, slots, tile, _ = blocks.shape
    n, m = lax.axis_size("col"), lax.axis_size("row")
    agg_row = aggregates.reshape(1, rows)
    dma = pltpu.SemaphoreType.DMA
    vmem = pl.BlockSpec(memory_space=pltpu.VMEM)
    hbm = pl.BlockSpec(memory_space=pltpu.HBM)
    galerkin, bound = pl.pallas_call(
        functools.partial(kernel, n, m),
        name="galerkin",
        out_shape=(
            jax.ShapeDtypeStruct((AGD, AGD * n, tile, tile), F32),
            jax.ShapeDtypeStruct((tile, tile), F32),
        ),
        in_specs=[hbm] * 5,
        out_specs=(vmem, vmem),
        scratch_shapes=[
            pltpu.VMEM((rows, slots), I32),
            pltpu.VMEM((1, rows), I32),
            pltpu.SMEM((rows, slots), I32),
            pltpu.SMEM((1, rows), I32),
            pltpu.SMEM((1, rows), I32),
            dma((5,)),
            pltpu.VMEM((rows, slots, tile, tile), F32),
            pltpu.VMEM((rows, tile, tile), F32),
            pltpu.VMEM((rows * slots + 1, tile, tile), F32),
            pltpu.VMEM((24, 128), I32),
            pltpu.VMEM((n, CAP, tile, tile), F32),
            pltpu.VMEM((n, CAP, tile, tile), F32),
            pltpu.VMEM((n, rows, slots), I32),
            pltpu.VMEM((n, 1, rows), I32),
            pltpu.VMEM((AGD * tile, tile), F32),
            pltpu.VMEM((8, 128), F32),
            pltpu.VMEM((n, 8, 128), F32),
            pltpu.VMEM((8, 128), F32),
            pltpu.VMEM((m, 8, 128), F32),
            pltpu.SMEM((24, 128), I32),
            dma((rows,)),
            dma,
            dma,
        ]
        + [dma((n,)) for _ in range(8)]
        + [dma((m,)) for _ in range(2)],
        compiler_params=pltpu.CompilerParams(
            collective_id=0, has_side_effects=True, vmem_limit_bytes=48 * 1024 * 1024
        ),
    )(*(pltpu.with_memory_space_constraint(x, pltpu.HBM) for x in (blocks, prolong, columns, agg_row, counts.reshape(1, rows))))
    return galerkin / (bound + 1e-06)


def solution(mesh):
    placed = (
        P(("row", "col"), None, None, None),
        P(("row", "col"), None, None),
        P(("row", "col")),
        P(("row", "col"), None),
        P(("row", "col")),
    )
    return jax.shard_map(
        per_device,
        mesh=mesh,
        in_specs=placed,
        out_specs=P(("row", "col"), None, None, None),
        check_vma=False,
    )
```

```python
import functools

import jax
import jax.numpy as jnp
from jax import lax
from jax.experimental import pallas as pl
from jax.experimental.pallas import tpu as pltpu
from jax.sharding import PartitionSpec as P

AGD = 2
CAP = 2
F32 = jnp.float32
BF16 = jnp.bfloat16
I32 = jnp.int32


def halves(x):
    high = x.astype(BF16)
    return high, (x - high.astype(F32)).astype(BF16)


def dot(a, b):
    return jnp.dot(a, b, preferred_element_type=F32)


def kernel(
    n, m, blocks_ref, prolong_ref, cols_ref, agg_ref, counts_ref,
    out_ref, bound_ref,
    cols_v, agg_v, cols_s, agg_s, counts_s, small_sem,
    blocks, prolong, partial, table, sent, got, cols_all, agg_all, rowsum, peak, peaks_col,
    peak2, peaks_row, table_s,
    block_sem, prolong_sem, table_sem, cols_send, cols_recv, agg_send, agg_recv,
    tile_send, tile_recv, pc_send, pc_recv, pr_send, pr_recv,
):
    rows, slots = cols_v.shape
    tile = prolong.shape[-1]
    none = rows * slots
    me = lax.axis_index("col")
    my_row = lax.axis_index("row")

    load_prolong = pltpu.make_async_copy(prolong_ref, prolong, prolong_sem)
    small = [
        pltpu.make_async_copy(src, dst, small_sem.at[at])
        for at, (src, dst) in enumerate(
            (
                (cols_ref, cols_v),
                (agg_ref, agg_v),
                (cols_ref, cols_s),
                (agg_ref, agg_s),
                (counts_ref, counts_s),
            )
        )
    ]
    for copy in small:
        copy.start()
    load_prolong.start()

    def load_block(i):
        return pltpu.make_async_copy(blocks_ref.at[i], blocks.at[i], block_sem.at[i])

    @pl.loop(0, rows)
    def _(i):
        load_block(i).start()

    def across(off):
        return lax.rem(me + off, n)

    def below(off):
        return lax.rem(my_row + off, m)

    barrier = pltpu.get_barrier_semaphore()

    @pl.loop(1, n)
    def _(off):
        pl.semaphore_signal(barrier, inc=1, device_id={"col": across(off)})

    @pl.loop(1, m)
    def _(off):
        pl.semaphore_signal(barrier, inc=1, device_id={"row": below(off)})

    for copy in small:
        copy.wait()
    pl.semaphore_wait(barrier, n + m - 2)

    def far_first(t):
        return n // 2 + (lax.rem(t, 2) * 2 - 1) * (t // 2)

    def send_cols(to, slot):
        return pltpu.make_async_remote_copy(
            cols_v, cols_all.at[slot], cols_send.at[to], cols_recv.at[slot], device_id={"col": to}
        )

    def send_agg(to, slot):
        return pltpu.make_async_remote_copy(
            agg_v, agg_all.at[slot], agg_send.at[to], agg_recv.at[slot], device_id={"col": to}
        )

    @pl.loop(1, n)
    def _(t):
        to = across(far_first(t))
        send_cols(to, me).start()

    @pl.loop(1, n)
    def _(t):
        send_agg(across(far_first(t)), me).start()

    sub = lax.broadcasted_iota(I32, (8, 128), 0)
    lane = lax.broadcasted_iota(I32, (8, 128), 1)
    keys = jnp.full((8, 128), -1, I32)
    for i in range(rows):
        for k in range(slots):
            here = (sub == i) & (lane == k)
            keys = jnp.where(here, cols_s[i, k] * AGD + agg_s[0, i], keys)
    order = sub * slots + lane

    def scan_keys(i, carry):
        prev, low, high = carry
        for k in range(slots):
            col = cols_s[i, k]
            s = i * slots + k
            owner, within = col // rows, lax.rem(col, rows)
            key = jnp.where(k < counts_s[0, i], col * AGD + agg_s[0, i], -2)
            prev = jnp.where((keys == key) & (order > s), s, prev)
            low = jnp.where(lane == owner, jnp.minimum(low, within), low)
            high = jnp.where(lane == owner, jnp.maximum(high, within), high)
        return prev, low, high

    prev, low, high = lax.fori_loop(
        0, rows, scan_keys,
        (jnp.full((8, 128), none, I32), jnp.full((8, 128), rows - 1, I32), jnp.zeros((8, 128), I32)),
    )
    wanted = jnp.where(lax.rem(sub, 2) == 0, low, jnp.where(high > low, high, -1))

    def scan_last(i, last):
        for k in range(slots):
            col = cols_s[i, k]
            owner, within = col // rows, lax.rem(col, rows)
            row = jnp.where(k < counts_s[0, i], agg_s[0, i], -1)
            hit = (lane == owner) & (sub // 2 == row) & (wanted == within)
            last = jnp.where(hit, i * slots + k, last)
        return last

    last = lax.fori_loop(0, rows, scan_last, jnp.full((8, 128), none, I32))
    table[0:8, :] = prev
    table[8:16, :] = last
    table[16:24, :] = jnp.where(sub == 0, low, high)
    to_scalars = pltpu.make_async_copy(table, table_s, table_sem)
    to_scalars.start()
    partial[none] = jnp.zeros((tile, tile), F32)
    agg_all[me] = agg_v[...]
    to_scalars.wait()

    load_prolong.wait()
    got[me, 0] = prolong[table_s[16, me]]
    got[me, 1] = prolong[table_s[17, me]]

    def send_tiles(to, slot):
        return pltpu.make_async_remote_copy(
            sent.at[to], got.at[slot], tile_send.at[to], tile_recv.at[slot], device_id={"col": to}
        )

    def reply(t, _):
        to = across(far_first(t))
        send_cols(to, to).wait_recv()
        asked = cols_all[to]
        mine = asked // rows == me
        within = lax.rem(asked, rows)
        sent[to, 0] = prolong[jnp.min(jnp.where(mine, within, rows - 1))]
        sent[to, 1] = prolong[jnp.max(jnp.where(mine, within, 0))]
        send_tiles(to, me).start()
        return 0

    lax.fori_loop(1, n, reply, 0)

    def first_product(i, _):
        load_block(i).wait()
        ph, pw = halves(prolong[i].T)
        lhs = jnp.concatenate([ph, pw, ph], axis=1)
        for k in range(0, slots, 2):
            ah, aw = halves(blocks[i, k])
            bh, bw = halves(blocks[i, k + 1])
            highs = jnp.concatenate([ah, bh], axis=1)
            rhs = jnp.concatenate([highs, highs, jnp.concatenate([aw, bw], axis=1)], axis=0)
            both = dot(lhs, rhs)
            s = i * slots + k
            partial[s] = both[:, :tile] + partial[table_s[i, k]]
            partial[s + 1] = both[:, tile:] + partial[table_s[i, k + 1]]
        return 0

    lax.fori_loop(0, rows, first_product, 0)

    rowsum[...] = jnp.zeros_like(rowsum)
    spot = lax.broadcasted_iota(I32, agg_v.shape, 1)

    def second_product(owner):
        lhs = jnp.concatenate(
            [
                jnp.concatenate([partial[table_s[8 + c * CAP + r, owner]] for r in range(CAP)], axis=1)
                for c in range(AGD)
            ],
            axis=0,
        )
        ids = agg_all[owner]
        right = []
        for r in range(CAP):
            one = jnp.max(jnp.where(spot == table_s[16 + r, owner], ids, 0)).astype(F32)
            p = got[owner, r]
            right.append(jnp.concatenate([p * (1.0 - one), p * one], axis=1))
        rhs = jnp.concatenate(right, axis=0)
        lh, lw = halves(lhs)
        rh, rw = halves(rhs)
        prod = dot(lh, rh) + dot(lh, rw) + dot(lw, rh)
        size = jnp.abs(prod)
        rowsum[...] += size[:, :tile] + size[:, tile:]
        for c in range(AGD):
            for a in range(AGD):
                out_ref[c, owner * AGD + a] = prod[
                    c * tile : (c + 1) * tile, a * tile : (a + 1) * tile
                ]

    second_product(me)

    def collect(t, _):
        owner = lax.rem(me - far_first(t) + n, n)
        send_agg(owner, owner).wait_recv()
        send_tiles(owner, owner).wait_recv()
        second_product(owner)
        return 0

    lax.fori_loop(1, n, collect, 0)

    most = jnp.max(jnp.sum(rowsum[...], axis=1, keepdims=True), axis=0, keepdims=True)
    peak[...] = jnp.broadcast_to(most, peak.shape)
    peaks_col[me] = jnp.broadcast_to(most, peak.shape)

    def send_peak(to, slot):
        return pltpu.make_async_remote_copy(
            peak, peaks_col.at[slot], pc_send.at[to], pc_recv.at[slot], device_id={"col": to}
        )

    def send_peak2(to, slot):
        return pltpu.make_async_remote_copy(
            peak2, peaks_row.at[slot], pr_send.at[to], pr_recv.at[slot], device_id={"row": to}
        )

    @pl.loop(1, n)
    def _(t):
        send_peak(across(far_first(t)), me).start()

    @pl.loop(1, n)
    def _(off):
        to = across(off)
        send_cols(to, me).wait_send()
        send_agg(to, me).wait_send()
        send_tiles(to, me).wait_send()

    @pl.loop(1, n)
    def _(off):
        send_peak(across(off), across(off)).wait_recv()

    over = jnp.max(peaks_col[...], axis=0)
    peak2[...] = over
    peaks_row[my_row] = over

    @pl.loop(1, m)
    def _(off):
        send_peak2(below(off), my_row).start()

    @pl.loop(1, m)
    def _(off):
        send_peak2(below(off), below(off)).wait_recv()

    bound_ref[...] = jnp.broadcast_to(
        jnp.max(peaks_row[...], axis=0)[:1, :1] + 1e-06, bound_ref.shape
    )

    @pl.loop(1, n)
    def _(off):
        send_peak(across(off), me).wait_send()

    @pl.loop(1, m)
    def _(off):
        send_peak2(below(off), my_row).wait_send()


def per_device(blocks, prolong, counts, columns, aggregates):
    rows, slots, tile, _ = blocks.shape
    n, m = lax.axis_size("col"), lax.axis_size("row")
    agg_row = aggregates.reshape(1, rows)
    dma = pltpu.SemaphoreType.DMA
    vmem = pl.BlockSpec(memory_space=pltpu.VMEM)
    hbm = pl.BlockSpec(memory_space=pltpu.HBM)
    galerkin, bound = pl.pallas_call(
        functools.partial(kernel, n, m),
        name="galerkin",
        out_shape=(
            jax.ShapeDtypeStruct((AGD, AGD * n, tile, tile), F32),
            jax.ShapeDtypeStruct((tile, tile), F32),
        ),
        in_specs=[hbm] * 5,
        out_specs=(vmem, vmem),
        scratch_shapes=[
            pltpu.VMEM((rows, slots), I32),
            pltpu.VMEM((1, rows), I32),
            pltpu.SMEM((rows, slots), I32),
            pltpu.SMEM((1, rows), I32),
            pltpu.SMEM((1, rows), I32),
            dma((5,)),
            pltpu.VMEM((rows, slots, tile, tile), F32),
            pltpu.VMEM((rows, tile, tile), F32),
            pltpu.VMEM((rows * slots + 1, tile, tile), F32),
            pltpu.VMEM((24, 128), I32),
            pltpu.VMEM((n, CAP, tile, tile), F32),
            pltpu.VMEM((n, CAP, tile, tile), F32),
            pltpu.VMEM((n, rows, slots), I32),
            pltpu.VMEM((n, 1, rows), I32),
            pltpu.VMEM((AGD * tile, tile), F32),
            pltpu.VMEM((8, 128), F32),
            pltpu.VMEM((n, 8, 128), F32),
            pltpu.VMEM((8, 128), F32),
            pltpu.VMEM((m, 8, 128), F32),
            pltpu.SMEM((24, 128), I32),
            dma((rows,)),
            dma,
            dma,
        ]
        + [dma((n,)) for _ in range(8)]
        + [dma((m,)) for _ in range(2)],
        compiler_params=pltpu.CompilerParams(
            collective_id=0, has_side_effects=True, vmem_limit_bytes=48 * 1024 * 1024
        ),
    )(*(pltpu.with_memory_space_constraint(x, pltpu.HBM) for x in (blocks, prolong, columns, agg_row, counts.reshape(1, rows))))
    return galerkin / bound


def solution(mesh):
    placed = (
        P(("row", "col"), None, None, None),
        P(("row", "col"), None, None),
        P(("row", "col")),
        P(("row", "col"), None),
        P(("row", "col")),
    )
    return jax.shard_map(
        per_device,
        mesh=mesh,
        in_specs=placed,
        out_specs=P(("row", "col"), None, None, None),
        check_vma=False,
    )
```
